32 devices in a mesh: seq: 8 (over z, x), panel: 4 (over y, core).
Axes of the slice: x: 2, y: 2, z: 4, core: 2. Of those that a mesh axis runs over, the one named last changes fastest.
Arguments:
- tokens: bfloat16 [512, 8192], P(('seq', 'panel')), may hold values from -6 to 6
- gate_weight: bfloat16 [2048, 8192], P(('seq', 'panel')), may hold values from -0.0625 to 0.0625
- up_weight: bfloat16 [2048, 8192], P(('seq', 'panel')), may hold values from -0.0625 to 0.0625
- gate_mask: int32 [32, 128], P(('seq', 'panel')), may hold values from 0 to 1, as said below
- up_mask: int32 [32, 128], P(('seq', 'panel')), may hold values from 0 to 1, as said below
Outputs:
- hidden: bfloat16 [512, 2048], P(('seq', 'panel'))
The draws below stay inside these ranges and needn't reach their ends.
Inputs may be any that keep to these rules, and one draw needn't show every extreme that they name: Every block row of gate_mask keeps between 32 and 96 of its 128 blocks; some block row keeps exactly 96. Every block row of up_mask keeps between 32 and 96 of its 128 blocks; some block row keeps exactly 96.
All inputs are finite; a program needn't handle non-finite values.
Results may differ from the reference program's by a relative error of at most 0.0012.
Values may be sent and summed in bfloat16 or wider, within the bound.
A program may use at most 128 MiB of HBM per device.

```python
import jax
import jax.numpy as jnp
from jax import lax

D = 8192
BLOCK = 64
FF = 2048
TOKENS = 512


def keep_blocks(key, row_blocks, col_blocks):
    key_count, key_top, key_rank = jax.random.split(key, 3)
    lowest = row_blocks // 4
    highest = 3 * row_blocks // 4
    counts = jax.random.randint(key_count, (col_blocks,), lowest, highest + 1)
    chosen = jax.random.randint(key_top, (), 0, col_blocks)
    counts = jnp.where(jnp.arange(col_blocks) == chosen, highest, counts)
    scores = jax.random.randint(key_rank, (row_blocks, col_blocks), 0, 1 << 20) * row_blocks + jnp.arange(row_blocks)[:, None]
    order = jnp.argsort(scores, axis=0, stable=True)
    ranks = jnp.argsort(order, axis=0, stable=True)
    return jnp.transpose((ranks < counts[None, :]).astype(jnp.int32))


def draw_gate_mask(key, part):
    return keep_blocks(jax.random.fold_in(key, 11), D // BLOCK, FF // BLOCK)


def draw_up_mask(key, part):
    return keep_blocks(jax.random.fold_in(key, 23), D // BLOCK, FF // BLOCK)


def block_scale(stream_key, shape, cuts, least, high):
    factor_of = 1.0
    for dim, shards_of in cuts:
        draws = jax.random.uniform(jax.random.fold_in(jax.random.fold_in(stream_key, 6), dim), (shards_of,), jnp.float32, least / len(cuts), high / len(cuts))
        factor_of = factor_of * jnp.repeat(jnp.exp(draws), shape[dim] // shards_of).reshape((-1,) + (1,) * (len(shape) - 1 - dim))
    return factor_of


def scatter_about(key, extent, deviation, limit, pieces=(), held_as=jnp.bfloat16):
    gain = block_scale(key, extent, pieces, -0.22, 0.18) if pieces else 1.0
    entries = jax.random.normal(key, extent, jnp.float32) * deviation * gain
    return jnp.minimum(jnp.maximum(entries, -limit), limit).astype(held_as)


def setup_inputs(seed: int = 0) -> dict:
    key_list = jax.random.split(jax.random.key(seed), 6)
    return {
        "tokens": scatter_about(key_list[0], (TOKENS, D), 1.0, 6.0, ((0, 32),)),
        "gate_weight": scatter_about(key_list[1], (FF, D), D ** -0.5, 0.0625, ((0, 32),)),
        "up_weight": scatter_about(key_list[2], (FF, D), D ** -0.5, 0.0625, ((0, 32),)),
        "gate_mask": draw_gate_mask(jax.random.fold_in(key_list[5], 71), 0),
        "up_mask": draw_up_mask(jax.random.fold_in(key_list[5], 71), 0),
    }


def expand_mask(mask, weight):
    block_rows = weight.shape[0] // mask.shape[0]
    block_cols = weight.shape[1] // mask.shape[1]
    full_mask = jnp.repeat(jnp.repeat(mask.astype(jnp.bfloat16), block_rows, axis=0), block_cols, axis=1)
    return weight * full_mask


def project(tokens, weight):
    return lax.dot_general(tokens, weight, (((1,), (1,)), ((), ())), preferred_element_type=jnp.float32)


def reference(tokens, gate_weight, up_weight, gate_mask, up_mask):
    gate = project(tokens, expand_mask(gate_mask, gate_weight))
    up_values = project(tokens, expand_mask(up_mask, up_weight))
    return (jax.nn.silu(gate) * up_values).astype(jnp.bfloat16)
```

```python
import functools

import jax
import jax.numpy as jnp
from jax import lax
from jax.experimental import pallas as pl
from jax.experimental.pallas import tpu as pltpu
from jax.sharding import PartitionSpec as P

MESH = pl.DeviceIdType.MESH
GROUPS = 4
NZ = 4
L, XA, XC, XB, YA, YC, YB, DA, DC, DB = range(10)
NKINDS = 10


def passed_along(block, axis, distance):
    devices = range(lax.axis_size(axis))
    route = [((i - distance) % len(devices), i) for i in devices]
    return lax.ppermute(block, axis, route)


def masked_weight(weight, mask):
    row_blocks, col_blocks = mask.shape
    shaped = weight.reshape(
        row_blocks, weight.shape[0] // row_blocks, col_blocks, weight.shape[1] // col_blocks
    )
    return (shaped * mask.astype(jnp.bfloat16)[:, None, :, None]).reshape(weight.shape)


def project(token_rows, weight):
    return lax.dot_general(
        token_rows, weight, (((1,), (1,)), ((), ())), preferred_element_type=jnp.float32
    )


def gated_block(token_rows, gate_part, up_part):
    gate = project(token_rows, gate_part)
    up_values = project(token_rows, up_part)
    return (jax.nn.silu(gate) * up_values).astype(jnp.bfloat16)


def collect_panels(stacked):
    panel_count = lax.axis_size("panel")
    collected = [(stacked, 0)]
    moving = stacked
    for distance in range(1, panel_count):
        moving = passed_along(moving, "panel", 1)
        collected.append((moving, distance))
    return collected


def general_shards(tokens, gate_weight, up_weight, gate_mask, up_mask):
    panel_count = lax.axis_size("panel")
    my_panel = lax.axis_index("panel")
    width_rows = gate_weight.shape[0]
    stacked = jnp.stack([masked_weight(gate_weight, gate_mask), masked_weight(up_weight, up_mask)])
    collected = collect_panels(stacked)
    gathered = lax.all_gather(tokens, "seq", axis=0, tiled=True)
    tile = jnp.zeros((gathered.shape[0], panel_count * width_rows), jnp.bfloat16)
    for pair, distance in collected:
        source = (my_panel - distance) % panel_count
        result = gated_block(gathered, pair[0], pair[1])
        tile = lax.dynamic_update_slice_in_dim(tile, result, source * width_rows, 1)
    return lax.all_to_all(tile, "seq", split_axis=0, concat_axis=1, tiled=True)


def kernel(
    tok, gw, uw, gm, um, out,
    held, w, masks, wide, acc, hid,
    recv_sem, send_sem, part_send, part_recv, local_sem, out_send, out_recv, out_local,
):
    rows, width = tok.shape
    wrows = gw.shape[0]
    nblocks = held.shape[0] // rows
    seq, panel = lax.axis_index("seq"), lax.axis_index("panel")
    z, x = seq // 2, seq % 2
    y, core = panel // 2, panel % 2
    gc = width // GROUPS
    unit = gc // 8

    def block_of(bz, bx, by):
        return (bz * 2 + bx) * 2 + by

    def device(bz, bx, by):
        return (bz * 2 + bx, by * 2 + core)

    me = block_of(z, x, y)
    xdev, ydev = device(z, 1 - x, y), device(z, x, 1 - y)
    updev, downdev = device(z + 1, x, y), device(z - 1, x, y)
    partner = (seq, y * 2 + 1 - core)

    barrier = pltpu.get_barrier_semaphore()
    for dev in (xdev, ydev, partner):
        pl.semaphore_signal(barrier, inc=1, device_id=dev, device_id_type=MESH)

    @pl.when(z < NZ - 1)
    def _():
        pl.semaphore_signal(barrier, inc=1, device_id=updev, device_id_type=MESH)

    @pl.when(z > 0)
    def _():
        pl.semaphore_signal(barrier, inc=1, device_id=downdev, device_id_type=MESH)

    rows_of = lambda b: pl.ds(pl.multiple_of(b * rows, rows), rows)
    own = pl.ds(pl.multiple_of(core * wrows, wrows), wrows)
    own_up = pl.ds(pl.multiple_of((2 + core) * wrows, wrows), wrows)
    locals_ = [
        pltpu.make_async_copy(gw, w.at[own], local_sem.at[0]),
        pltpu.make_async_copy(uw, w.at[own_up], local_sem.at[1]),
        pltpu.make_async_copy(gm, masks.at[core], local_sem.at[2]),
        pltpu.make_async_copy(um, masks.at[2 + core], local_sem.at[3]),
        pltpu.make_async_copy(tok, held.at[rows_of(me)], local_sem.at[4]),
    ]
    for copy in locals_:
        copy.start()

    links = (z > 0).astype(jnp.int32) + (z < NZ - 1).astype(jnp.int32)
    pl.semaphore_wait(barrier, 3 + links)

    def cols(g, first, last):
        return pl.ds(g * gc + first * unit, (last - first) * unit)

    ALL, A, B, C = (0, 8), (0, 3), (3, 5), (5, 8)
    AB, BC = (0, 4), (4, 8)
    sends = []

    def when(cond):
        return pl.when(cond) if cond is not None else (lambda f: f())

    def send(g, origin, part, dev, kind, oz, cond=None):
        index = len(sends)
        span = cols(g, *part)
        src = tok.at[:, span] if origin is None else held.at[rows_of(origin), span]
        at = me if origin is None else origin
        copy = pltpu.make_async_remote_copy(
            src_ref=src, dst_ref=held.at[rows_of(at), span],
            send_sem=send_sem.at[index], recv_sem=recv_sem.at[g, kind, oz],
            device_id=dev, device_id_type=MESH,
        )
        sends.append((copy, cond))
        when(cond)(copy.start)

    def await_piece(g, origin, part, kind, oz):
        ref = held.at[rows_of(origin), cols(g, *part)]
        pltpu.make_async_copy(ref, ref, recv_sem.at[g, kind, oz]).wait()

    has_up, has_down = z < NZ - 1, z > 0

    def phase0(g):
        send(g, None, ALL, updev, L, z, has_up)
        send(g, None, ALL, downdev, L, z, has_down)
        send(g, None, ALL, xdev, XA, z)
        send(g, None, ALL, ydev, YA, z)

    def plane(g):
        bx, by = block_of(z, 1 - x, y), block_of(z, x, 1 - y)
        await_piece(g, bx, ALL, XA, z)
        send(g, bx, AB, ydev, DA, z)
        send(g, bx, B, updev, XB, z, has_up)
        send(g, bx, B, downdev, XB, z, has_down)
        await_piece(g, by, ALL, YA, z)
        send(g, by, BC, xdev, DC, z)
        send(g, by, B, updev, YB, z, has_up)
        send(g, by, B, downdev, YB, z, has_down)

    def plane_diagonal(g):
        bd = block_of(z, 1 - x, 1 - y)
        await_piece(g, bd, AB, DA, z)
        await_piece(g, bd, BC, DC, z)
        send(g, bd, B, updev, DB, z, has_up)
        send(g, bd, B, downdev, DB, z, has_down)

    def sides(d):
        if d < 1 or d > NZ - 1:
            return
        for up in (True, False):
            oz = z - d if up else z + d
            here = oz >= 0 if up else oz <= NZ - 1
            onward = jnp.logical_and(here, has_up if up else has_down)
            yield oz, here, (updev if up else downdev), (onward if d < NZ - 1 else False)

    def line(g, d):
        for oz, here, dev, onward in sides(d):
            b = block_of(oz, x, y)
            when(here)(functools.partial(await_piece, g, b, ALL, L, oz))
            if onward is not False:
                send(g, b, ALL, dev, L, oz, onward)
            send(g, b, A, xdev, XA, oz, here)
            send(g, b, C, ydev, YC, oz, here)
            send(g, b, C, xdev, XC, oz, here)
            send(g, b, A, ydev, YA, oz, here)

    def cross(g, d):
        for oz, here, dev, onward in sides(d):
            bx, by = block_of(oz, 1 - x, y), block_of(oz, x, 1 - y)
            when(here)(functools.partial(await_piece, g, bx, A, XA, oz))
            send(g, bx, A, ydev, DA, oz, here)
            when(here)(functools.partial(await_piece, g, by, C, YC, oz))
            send(g, by, C, xdev, DC, oz, here)

    def ride(g, d, which):
        for oz, here, dev, onward in sides(d):
            for kind, flip in which:
                b = block_of(oz, 1 - x if flip[0] else x, 1 - y if flip[1] else y)
                when(here)(functools.partial(await_piece, g, b, B, kind, oz))
                if onward is not False:
                    send(g, b, B, dev, kind, oz, onward)

    XY = ((XB, (1, 0)), (YB, (0, 1)))
    DD = ((DB, (1, 1)),)

    def leaves(g):
        for d in range(1, NZ):
            for oz, here, _, _ in sides(d):
                def rest(oz=oz):
                    await_piece(g, block_of(oz, 1 - x, y), C, XC, oz)
                    await_piece(g, block_of(oz, x, 1 - y), A, YA, oz)
                    await_piece(g, block_of(oz, 1 - x, 1 - y), A, DA, oz)
                    await_piece(g, block_of(oz, 1 - x, 1 - y), C, DC, oz)
                when(here)(rest)

    def multiply(g):
        span = cols(g, 0, 8)
        part = lax.dot_general(
            held[:, span], w[:, span], (((1,), (1,)), ((), ())), preferred_element_type=jnp.float32
        )
        acc[...] = part if g == 0 else acc[...] + part

    def phase(g, p):
        if p == 0:
            phase0(g)
        elif p == 1:
            plane(g)
            line(g, 1)
        elif p == 2:
            plane_diagonal(g)
            line(g, 2)
            ride(g, 1, XY)
            cross(g, 1)
        elif p == 3:
            line(g, 3)
            ride(g, 1, DD)
            ride(g, 2, XY)
            cross(g, 2)
        elif p == 4:
            ride(g, 2, DD)
            ride(g, 3, XY)
            cross(g, 3)
        else:
            ride(g, 3, DD)
            leaves(g)
            multiply(g)

    def weights():
        copies = []
        for i, (src, dst) in enumerate((
            (gw, w.at[own]), (uw, w.at[own_up]), (gm, masks.at[core]), (um, masks.at[2 + core]),
        )):
            copies.append(pltpu.make_async_remote_copy(
                src_ref=src, dst_ref=dst, send_sem=part_send.at[i], recv_sem=part_recv.at[i],
                device_id=partner, device_id_type=MESH,
            ))
        for copy in copies:
            copy.start()
        return copies

    def prune(copies):
        for copy in copies:
            copy.wait()
        for copy in locals_:
            copy.wait()
        step = 512
        block = width // masks.shape[2]
        row = lax.broadcasted_iota(jnp.int32, (8, masks.shape[2]), 0)
        table = jnp.zeros((8, masks.shape[2]), jnp.float32)
        for r in range(4):
            table = jnp.where(row == r, masks[r].astype(jnp.float32), table)
        table = table.astype(jnp.bfloat16)

        @pl.loop(0, width // step)
        def _(i):
            start = pl.multiple_of(i * step, step)
            where_ = lax.broadcasted_iota(jnp.int32, (masks.shape[2], step), 0)
            col = lax.broadcasted_iota(jnp.int32, (masks.shape[2], step), 1) + start
            first = where_ * block
            inside = jnp.logical_and(col >= first, col < first + block)
            select = jnp.where(inside, 1.0, 0.0).astype(jnp.bfloat16)
            wide[...] = jnp.dot(table, select, preferred_element_type=jnp.float32)
            for r in range(4):
                at = (pl.ds(r * wrows, wrows), pl.ds(start, step))
                keep = jnp.broadcast_to(wide[r:r + 1, :], (wrows, step))
                w[at] = (w[at].astype(jnp.float32) * keep).astype(jnp.bfloat16)

    for s in range(GROUPS + 5):
        for g in range(GROUPS):
            if 0 <= s - g <= 5:
                phase(g, s - g)
        if s == 0:
            copies = weights()
        if s == 1:
            prune(copies)

    half = acc.shape[1] // 2
    gate = acc[:, :half]
    hid[...] = (gate / (1.0 + jnp.exp(-gate)) * acc[:, half:]).astype(jnp.bfloat16)
    mine = pl.ds(pl.multiple_of(me * half, half), half)
    keep_own = pltpu.make_async_copy(hid.at[rows_of(me)], out.at[:, mine], out_local)
    results = []
    for k in range(nblocks - 1, 0, -1):
        dz, dx, dy = k // 4, (k // 2) % 2, k % 2
        tz, tx, ty = (z + dz) % NZ, (x + dx) % 2, (y + dy) % 2
        target = block_of(tz, tx, ty)
        copy = pltpu.make_async_remote_copy(
            src_ref=hid.at[rows_of(target)], dst_ref=out.at[:, mine],
            send_sem=out_send.at[k], recv_sem=out_recv.at[k],
            device_id=device(tz, tx, ty), device_id_type=MESH,
        )
        copy.start()
        results.append(k)
    keep_own.start()
    for copy, cond in sends:
        when(cond)(copy.wait_send)
    for k in results:
        dz, dx, dy = k // 4, (k // 2) % 2, k % 2
        source = block_of((z + NZ - dz) % NZ, (x + dx) % 2, (y + dy) % 2)
        ref = out.at[:, pl.ds(pl.multiple_of(source * half, half), half)]
        pltpu.make_async_copy(ref, ref, out_recv.at[k]).wait()
        sent = hid.at[rows_of(source)]
        pltpu.make_async_copy(sent, sent, out_send.at[k]).wait()
    keep_own.wait()


NSENDS = GROUPS * 64


def shards(tokens, gate_weight, up_weight, gate_mask, up_mask):
    rows, width = tokens.shape
    wrows = gate_weight.shape[0]
    blocks = lax.axis_size("seq") * lax.axis_size("panel") // 2
    hidden = lax.axis_size("seq") * lax.axis_size("panel") * wrows
    dma = pltpu.SemaphoreType.DMA
    return pl.pallas_call(
        kernel,
        out_shape=jax.ShapeDtypeStruct((rows, hidden), jnp.bfloat16),
        in_specs=[pl.BlockSpec(memory_space=pl.ANY)] * 5,
        out_specs=pl.BlockSpec(memory_space=pl.ANY),
        scratch_shapes=[
            pltpu.VMEM((blocks * rows, width), jnp.bfloat16),
            pltpu.VMEM((4 * wrows, width), jnp.bfloat16),
            pltpu.VMEM((4, 1, gate_mask.shape[1]), jnp.int32),
            pltpu.VMEM((8, 512), jnp.float32),
            pltpu.VMEM((blocks * rows, 4 * wrows), jnp.float32),
            pltpu.VMEM((blocks * rows, 2 * wrows), jnp.bfloat16),
            dma((GROUPS, NKINDS, NZ)),
            dma((NSENDS,)),
            dma((4,)), dma((4,)), dma((5,)),
            dma((blocks,)), dma((blocks,)), dma,
        ],
        compiler_params=pltpu.CompilerParams(collective_id=0, has_side_effects=True),
    )(tokens, gate_weight, up_weight, gate_mask, up_mask)


def solution(mesh):
    spec = P(("seq", "panel"), None)
    fits = mesh.shape["seq"] == 2 * NZ and mesh.shape["panel"] == 4
    body = shards if fits else general_shards
    return jax.shard_map(
        body, mesh=mesh, in_specs=(spec,) * 5, out_specs=spec, check_vma=False
    )
```

```python
import functools

import jax
import jax.numpy as jnp
from jax import lax
from jax.experimental import pallas as pl
from jax.experimental.pallas import tpu as pltpu
from jax.sharding import PartitionSpec as P

MESH = pl.DeviceIdType.MESH
RIDING = 14
NZ = 4
L, LC, X, X2, Y, Y2, DA, DC, R, R2 = range(10)
NKINDS = 10


def passed_along(block, axis, distance):
    devices = range(lax.axis_size(axis))
    route = [((i - distance) % len(devices), i) for i in devices]
    return lax.ppermute(block, axis, route)


def masked_weight(weight, mask):
    row_blocks, col_blocks = mask.shape
    shaped = weight.reshape(
        row_blocks, weight.shape[0] // row_blocks, col_blocks, weight.shape[1] // col_blocks
    )
    return (shaped * mask.astype(jnp.bfloat16)[:, None, :, None]).reshape(weight.shape)


def project(token_rows, weight):
    return lax.dot_general(
        token_rows, weight, (((1,), (1,)), ((), ())), preferred_element_type=jnp.float32
    )


def gated_block(token_rows, gate_part, up_part):
    gate = project(token_rows, gate_part)
    up_values = project(token_rows, up_part)
    return (jax.nn.silu(gate) * up_values).astype(jnp.bfloat16)


def collect_panels(stacked):
    panel_count = lax.axis_size("panel")
    collected = [(stacked, 0)]
    moving = stacked
    for distance in range(1, panel_count):
        moving = passed_along(moving, "panel", 1)
        collected.append((moving, distance))
    return collected


def general_shards(tokens, gate_weight, up_weight, gate_mask, up_mask):
    panel_count = lax.axis_size("panel")
    my_panel = lax.axis_index("panel")
    width_rows = gate_weight.shape[0]
    stacked = jnp.stack([masked_weight(gate_weight, gate_mask), masked_weight(up_weight, up_mask)])
    collected = collect_panels(stacked)
    gathered = lax.all_gather(tokens, "seq", axis=0, tiled=True)
    tile = jnp.zeros((gathered.shape[0], panel_count * width_rows), jnp.bfloat16)
    for pair, distance in collected:
        source = (my_panel - distance) % panel_count
        result = gated_block(gathered, pair[0], pair[1])
        tile = lax.dynamic_update_slice_in_dim(tile, result, source * width_rows, 1)
    return lax.all_to_all(tile, "seq", split_axis=0, concat_axis=1, tiled=True)


def kernel(
    tok, gw, uw, gm, um, out,
    held, w, masks, wide, hid,
    recv_sem, send_sem, part_send, part_recv, local_sem, out_send, out_recv, out_local,
):
    rows, width = tok.shape
    wrows = gw.shape[0]
    seq, panel = lax.axis_index("seq"), lax.axis_index("panel")
    z, x = seq // 2, seq % 2
    y, core = panel // 2, panel % 2
    def block_of(bz, bx, by):
        return (bz * 2 + bx) * 2 + by

    def device(bz, bx, by):
        return (bz * 2 + bx, by * 2 + core)

    me = block_of(z, x, y)
    xdev, ydev = device(z, 1 - x, y), device(z, x, 1 - y)
    updev, downdev = device(z + 1, x, y), device(z - 1, x, y)
    partner = (seq, y * 2 + 1 - core)

    barrier = pltpu.get_barrier_semaphore()
    for dev in (xdev, ydev, partner):
        pl.semaphore_signal(barrier, inc=1, device_id=dev, device_id_type=MESH)

    @pl.when(z < NZ - 1)
    def _():
        pl.semaphore_signal(barrier, inc=1, device_id=updev, device_id_type=MESH)

    @pl.when(z > 0)
    def _():
        pl.semaphore_signal(barrier, inc=1, device_id=downdev, device_id_type=MESH)

    rows_of = lambda b: pl.ds(pl.multiple_of(b * rows, rows), rows)
    own = pl.ds(pl.multiple_of(core * wrows, wrows), wrows)
    own_up = pl.ds(pl.multiple_of((2 + core) * wrows, wrows), wrows)
    locals_ = [
        pltpu.make_async_copy(gw, w.at[own], local_sem.at[0]),
        pltpu.make_async_copy(uw, w.at[own_up], local_sem.at[1]),
        pltpu.make_async_copy(gm, masks.at[core], local_sem.at[2]),
        pltpu.make_async_copy(um, masks.at[2 + core], local_sem.at[3]),
        pltpu.make_async_copy(tok, held.at[rows_of(me)], local_sem.at[4]),
    ]
    for copy in locals_:
        copy.start()

    links = (z > 0).astype(jnp.int32) + (z < NZ - 1).astype(jnp.int32)
    pl.semaphore_wait(barrier, 3 + links)

    unit = width // 64
    first = (64 - RIDING) // 2
    ALL, C, A, B = (0, 64), (0, first), (first, 64 - RIDING), (64 - RIDING, 64)
    AB = (first, 64)
    RIDES = (((64 - RIDING, 64 - RIDING // 2), R), ((64 - RIDING // 2, 64), R2))
    sends = []

    def when(cond):
        return pl.when(cond) if cond is not None else (lambda f: f())

    def cols(part):
        return pl.ds(part[0] * unit, (part[1] - part[0]) * unit)

    def plane_rows(oz):
        return pl.ds(pl.multiple_of(oz * 4 * rows, 4 * rows), 4 * rows)

    def copy_piece(src, at, part, dev, kind, oz, cond):
        span = cols(part)
        copy = pltpu.make_async_remote_copy(
            src_ref=src.at[:, span] if src is tok else src.at[at, span], dst_ref=held.at[at, span],
            send_sem=send_sem.at[len(sends)], recv_sem=recv_sem.at[kind, oz],
            device_id=dev, device_id_type=MESH,
        )
        sends.append((copy, cond))
        when(cond)(copy.start)

    def send(origin, part, dev, kind, oz, cond=None):
        copy_piece(held, rows_of(origin), part, dev, kind, oz, cond)

    def await_rows(at, part, kind, oz):
        ref = held.at[at, cols(part)]
        pltpu.make_async_copy(ref, ref, recv_sem.at[kind, oz]).wait()

    def await_piece(origin, part, kind, oz):
        await_rows(rows_of(origin), part, kind, oz)

    has_up, has_down = z < NZ - 1, z > 0
    at_end = jnp.logical_or(z == 0, z == NZ - 1)
    bx, by, bd = block_of(z, 1 - x, y), block_of(z, x, 1 - y), block_of(z, 1 - x, 1 - y)

    def begin():
        mine = rows_of(me)
        for part, kind in ((A, L), (C, LC)):
            copy_piece(tok, mine, part, updev, kind, z, has_up)
            copy_piece(tok, mine, part, downdev, kind, z, has_down)
        copy_piece(tok, mine, AB, xdev, X, z, None)
        copy_piece(tok, mine, C, ydev, Y, z, None)
        copy_piece(tok, mine, C, xdev, X2, z, None)
        copy_piece(tok, mine, AB, ydev, Y2, z, None)

    def plane():
        await_piece(by, C, Y, z)
        send(by, C, xdev, DC, z)
        await_piece(bx, AB, X, z)
        send(bx, AB, ydev, DA, z)

    def ride_own():
        await_piece(by, AB, Y2, z)
        await_piece(bd, AB, DA, z)
        for part, kind in RIDES:
            copy_piece(held, plane_rows(z), part, updev, kind, z, has_up)
            copy_piece(held, plane_rows(z), part, downdev, kind, z, has_down)

    def sides(d):
        for up in (True, False):
            oz = z - d if up else z + d
            here = oz >= 0 if up else oz <= NZ - 1
            onward = jnp.logical_and(here, has_up if up else has_down)
            yield oz, here, (updev if up else downdev), (onward if d < NZ - 1 else False)

    def line(d):
        for oz, here, dev, onward in sides(d):
            b = block_of(oz, x, y)
            when(here)(functools.partial(await_piece, b, A, L, oz))
            if onward is not False:
                send(b, A, dev, L, oz, onward)
            send(b, A, xdev, X, oz, here)
            when(here)(functools.partial(await_piece, b, C, LC, oz))
            if onward is not False:
                send(b, C, dev, LC, oz, onward)
            send(b, C, ydev, Y, oz, here)
            send(b, C, xdev, X2, oz, here)
            send(b, A, ydev, Y2, oz, here)

    def cross(d):
        for oz, here, dev, onward in sides(d):
            ox, oy = block_of(oz, 1 - x, y), block_of(oz, x, 1 - y)
            when(here)(functools.partial(await_piece, ox, A, X, oz))
            send(ox, A, ydev, DA, oz, here)
            when(here)(functools.partial(await_piece, oy, C, Y, oz))
            send(oy, C, xdev, DC, oz, here)

    def ride(d):
        for oz, here, dev, onward in sides(d):
            for part, kind in RIDES:
                when(here)(functools.partial(await_rows, plane_rows(oz), part, kind, oz))
                if onward is not False:
                    copy_piece(held, plane_rows(oz), part, dev, kind, oz, onward)

    half = 2 * wrows
    mine_out = pl.ds(pl.multiple_of(me * half, half), half)

    def result_copy(oz, k):
        tx, ty = (x + k // 2) % 2, (y + k % 2) % 2
        return pltpu.make_async_remote_copy(
            src_ref=hid.at[rows_of(block_of(oz, tx, ty))], dst_ref=out.at[:, mine_out],
            send_sem=out_send.at[oz, k], recv_sem=out_recv.at[z, k],
            device_id=device(oz, tx, ty), device_id_type=MESH,
        )

    def multiply(oz):
        both = lax.dot_general(
            held[plane_rows(oz), :], w[...], (((1,), (1,)), ((), ())), preferred_element_type=jnp.float32
        )
        gate = both[:, :half]
        hid[plane_rows(oz), :] = (gate / (1.0 + jnp.exp(-gate)) * both[:, half:]).astype(jnp.bfloat16)

    def own_plane():
        await_piece(bx, C, X2, z)
        await_piece(bd, C, DC, z)
        multiply(z)
        for k in (3, 2, 1):
            result_copy(z, k).start()

    def other_planes(d, cond=None):
        for oz, here, _, _ in sides(d):
            def finish(oz=oz):
                diagonal = block_of(oz, 1 - x, 1 - y)
                await_piece(block_of(oz, 1 - x, y), C, X2, oz)
                await_piece(block_of(oz, x, 1 - y), A, Y2, oz)
                await_piece(diagonal, A, DA, oz)
                await_piece(diagonal, C, DC, oz)
                multiply(oz)
                for k in (3, 2, 1, 0):
                    result_copy(oz, k).start()
            when(here if cond is None else jnp.logical_and(here, cond))(finish)

    def weights():
        copies = []
        for i, (src, dst) in enumerate((
            (gw, w.at[own]), (uw, w.at[own_up]), (gm, masks.at[core]), (um, masks.at[2 + core]),
        )):
            copies.append(pltpu.make_async_remote_copy(
                src_ref=src, dst_ref=dst, send_sem=part_send.at[i], recv_sem=part_recv.at[i],
                device_id=partner, device_id_type=MESH,
            ))
        for copy in copies:
            copy.start()
        return copies

    def prune(copies):
        for copy in copies:
            copy.wait()
        for copy in locals_:
            copy.wait()
        step = 512
        block = width // masks.shape[2]
        row = lax.broadcasted_iota(jnp.int32, (8, masks.shape[2]), 0)
        table = jnp.zeros((8, masks.shape[2]), jnp.float32)
        for r in range(4):
            table = jnp.where(row == r, masks[r].astype(jnp.float32), table)
        table = table.astype(jnp.bfloat16)

        @pl.loop(0, width // step)
        def _(i):
            start = pl.multiple_of(i * step, step)
            where_ = lax.broadcasted_iota(jnp.int32, (masks.shape[2], step), 0)
            col = lax.broadcasted_iota(jnp.int32, (masks.shape[2], step), 1) + start
            first = where_ * block
            inside = jnp.logical_and(col >= first, col < first + block)
            select = jnp.where(inside, 1.0, 0.0).astype(jnp.bfloat16)
            wide[...] = jnp.dot(table, select, preferred_element_type=jnp.float32)
            for r in range(4):
                at = (pl.ds(r * wrows, wrows), pl.ds(start, step))
                keep = jnp.broadcast_to(wide[r:r + 1, :], (wrows, step))
                w[at] = (w[at].astype(jnp.float32) * keep).astype(jnp.bfloat16)

    begin()
    swaps = weights()
    plane()
    line(1)
    prune(swaps)
    line(2)
    ride_own()
    cross(1)
    line(3)
    own_plane()
    ride(1)
    cross(2)
    other_planes(1, at_end)
    ride(2)
    other_planes(1, jnp.logical_not(at_end))
    cross(3)
    other_planes(2)
    ride(3)
    other_planes(3)

    keep_own = pltpu.make_async_copy(hid.at[rows_of(me)], out.at[:, mine_out], out_local)
    keep_own.start()
    for copy, cond in sends:
        when(cond)(copy.wait_send)
    for oz in range(NZ):
        for k in range(4):
            def settle(oz=oz, k=k):
                sent = hid.at[rows_of(block_of(oz, (x + k // 2) % 2, (y + k % 2) % 2))]
                pltpu.make_async_copy(sent, sent, out_send.at[oz, k]).wait()
                source = block_of(oz, (x + k // 2) % 2, (y + k % 2) % 2)
                ref = out.at[:, pl.ds(pl.multiple_of(source * half, half), half)]
                pltpu.make_async_copy(ref, ref, out_recv.at[oz, k]).wait()
            when(z != oz if k == 0 else None)(settle)
    keep_own.wait()


NSENDS = 68


def shards(tokens, gate_weight, up_weight, gate_mask, up_mask):
    rows, width = tokens.shape
    wrows = gate_weight.shape[0]
    blocks = lax.axis_size("seq") * lax.axis_size("panel") // 2
    hidden = lax.axis_size("seq") * lax.axis_size("panel") * wrows
    dma = pltpu.SemaphoreType.DMA
    return pl.pallas_call(
        kernel,
        out_shape=jax.ShapeDtypeStruct((rows, hidden), jnp.bfloat16),
        in_specs=[pl.BlockSpec(memory_space=pl.ANY)] * 5,
        out_specs=pl.BlockSpec(memory_space=pl.ANY),
        scratch_shapes=[
            pltpu.VMEM((blocks * rows, width), jnp.bfloat16),
            pltpu.VMEM((4 * wrows, width), jnp.bfloat16),
            pltpu.VMEM((4, 1, gate_mask.shape[1]), jnp.int32),
            pltpu.VMEM((8, 512), jnp.float32),
            pltpu.VMEM((blocks * rows, 2 * wrows), jnp.bfloat16),
            dma((NKINDS, NZ)),
            dma((NSENDS,)),
            dma((4,)), dma((4,)), dma((5,)),
            dma((NZ, 4)), dma((NZ, 4)), dma,
        ],
        compiler_params=pltpu.CompilerParams(collective_id=0, has_side_effects=True),
    )(tokens, gate_weight, up_weight, gate_mask, up_mask)


def solution(mesh):
    spec = P(("seq", "panel"), None)
    fits = mesh.shape["seq"] == 2 * NZ and mesh.shape["panel"] == 4
    body = shards if fits else general_shards
    return jax.shard_map(
        body, mesh=mesh, in_specs=(spec,) * 5, out_specs=spec, check_vma=False
    )
```
